128 devices in a mesh: grp: 4 (over y), dom: 32 (over z, x, core).
Axes of the slice: x: 4, y: 4, z: 4, core: 2. Of those that a mesh axis runs over, the one named last changes fastest.
Arguments:
- fields: float32 [210, 131072], P(None, ('grp', 'dom')), may hold values from -6 to 6
- metric: float32 [9, 131072], P(None, ('grp', 'dom')), may hold values from -5 to 5
- normals: float32 [12, 131072], P(None, ('grp', 'dom')), may hold values from -3 to 3
- fscale: float32 [4, 131072], P(None, ('grp', 'dom')), may hold values from 0.5 to 4
- orders: int32 [131072], P(('grp', 'dom')), may hold values from 1 to 4, as said below
- slots: int32 [131072], P(('grp', 'dom')), may hold values from 0 to 511, as said below
- send_faces: int32 [1179648], P(('grp', 'dom')), may hold values from 0 to 8192, as said below
- recv_faces: int32 [1048576], P(('grp', 'dom')), may hold values from 0 to 9216, as said below
- dmat: float32 [4, 105, 35], P('grp'), may hold values from -4 to 4
- tmat: float32 [4, 60, 35], P('grp'), may hold values from -4 to 4
- lmat: float32 [4, 35, 60], P('grp'), may hold values from -3 to 3
Outputs:
- rhs: float32 [210, 262144], P(None, ('grp', 'dom'))
The draws below stay inside these ranges and needn't reach their ends.
Inputs may be any that keep to these rules, and one draw needn't show every extreme that they name: `orders`: on each device every order from 1 to 4 is held by at least one element and by at most 512; one order is held by exactly 512. The elements of one device that share an order have distinct slots. `send_faces`: each entry names a face of an occupied slot of the sending bucket or equals 4 * 2048 (nothing); in each list the items in use stand first. `recv_faces`: every face of an occupied slot names a distinct received item that is in use, and every item in use is named by exactly one face; faces of empty slots hold 9216. A list carries at most 768 items in use, and some list carries exactly 768.
All inputs are finite; a program needn't handle non-finite values.
Results may differ from the reference program's by a relative error of at most 0.0003.
Values sent between devices are 32-bit elements; how exact they have to be, the bound alone decides.
No kernel may reach another device: no remote copies, remote signals or barrier semaphores. Data moves between devices by JAX's collectives and lax.ppermute only.
A program may use at most 128 MiB of HBM per device.

```python
import math
import jax
import jax.numpy as jnp
from jax import lax

NPM = 35
FPTS = 15
ORDERS = 4
E_DEV = 1024
CAP = 512
NB = 2048
FCAP = 768
LISTS = 9216
DOMS = 32
ELEMS = 131072
SLOTS = 262144
DEVICES = 128


def mesh_tables(key):
    base = jax.random.fold_in(key, 4242)
    streams = jax.random.split(base, 7)
    spare = E_DEV - CAP
    leading = jax.random.randint(streams[0], (DEVICES,), 0, ORDERS)
    cuts = jax.random.randint(streams[1], (DEVICES, 2), 0, spare - 2)
    lower = jnp.minimum(cuts[:, 0], cuts[:, 1]) + 1
    upper = jnp.maximum(cuts[:, 0], cuts[:, 1]) + 2
    rank_sizes = jnp.stack([jnp.full((DEVICES,), CAP, jnp.int32), lower, upper - lower, spare - upper], 1)
    rank_ends = jnp.cumsum(rank_sizes, 1)
    rank_starts = rank_ends - rank_sizes
    position = jax.vmap(lambda sub_key: jax.random.permutation(sub_key, E_DEV))(jax.random.split(streams[2], DEVICES)).astype(jnp.int32)
    rank_of = jnp.sum((position[:, :, None] >= rank_ends[:, None, :]).astype(jnp.int32), 2)
    within = position - jnp.take_along_axis(rank_starts, rank_of, 1)
    order_index = (leading[:, None] + rank_of) % ORDERS
    shuffles = jax.vmap(lambda sub_key: jax.random.permutation(sub_key, CAP))(jax.random.split(streams[3], DEVICES * ORDERS)).astype(jnp.int32)
    shuffles = shuffles.reshape(DEVICES, ORDERS * CAP)
    slot_value = jnp.take_along_axis(shuffles, order_index * CAP + within, 1)
    device_ids = jnp.arange(DEVICES, dtype=jnp.int32)[:, None]
    bucket_dev = order_index * DOMS + device_ids % DOMS
    bucket_col = device_ids // DOMS * CAP + slot_value
    occupied = jnp.zeros((DEVICES, NB), jnp.int32).at[bucket_dev, bucket_col].set(1)
    face_total = 4 * jnp.sum(occupied, 1)
    occupied_slots = jnp.argsort((1 - occupied) * NB + jnp.arange(NB, dtype=jnp.int32)[None], axis=1).astype(jnp.int32)
    enumerated = jnp.arange(4 * NB, dtype=jnp.int32)
    face_of = (enumerated % 4)[None] * NB + occupied_slots[:, enumerated // 4]
    valid = enumerated[None] < face_total[:, None]
    list_total = 3 * ORDERS
    first_list = jax.random.randint(streams[4], (DEVICES,), 0, list_total)
    leading_count = jnp.minimum(face_total, FCAP)
    remainder = face_total - leading_count
    share = remainder // (list_total - 1)
    extra = remainder % (list_total - 1)
    offset = (jnp.arange(list_total, dtype=jnp.int32)[None] - first_list[:, None]) % list_total
    counts = jnp.where(offset == 0, leading_count[:, None], share[:, None] + (offset - 1 < extra[:, None]).astype(jnp.int32))
    list_ends = jnp.cumsum(counts, 1)
    list_starts = list_ends - counts
    face_shuffle = jax.vmap(lambda sub_key: jax.random.permutation(sub_key, 4 * NB))(jax.random.split(streams[5], DEVICES)).astype(jnp.int32)
    scores = jnp.where(valid, face_shuffle, 4 * NB + enumerated[None])
    ranking = jnp.argsort(jnp.argsort(scores, axis=1), axis=1).astype(jnp.int32)
    list_of = jnp.sum((ranking[:, :, None] >= list_ends[:, None, :]).astype(jnp.int32), 2)
    list_of = jnp.minimum(list_of, list_total - 1)
    place_in = ranking - jnp.take_along_axis(list_starts, list_of, 1)
    entry_value = jnp.where(valid, list_of * FCAP + place_in, LISTS)
    targets = jnp.where(valid, face_of, 4 * NB)
    receive = jnp.full((DEVICES, 4 * NB + 1), LISTS, jnp.int32).at[device_ids, targets].set(entry_value)[:, :4 * NB]
    sender_ids = jnp.arange(DEVICES, dtype=jnp.int32)[:, None, None]
    direction = jnp.arange(3, dtype=jnp.int32)[None, :, None]
    peer_group = jnp.arange(ORDERS, dtype=jnp.int32)[None, None, :]
    receiver = peer_group * DOMS + (sender_ids % DOMS + direction - 1) % DOMS
    list_index = direction * ORDERS + sender_ids // DOMS
    wanted = counts[receiver, list_index]
    picks = jax.random.randint(streams[6], (DEVICES, 3, ORDERS, FCAP), 0, 2 ** 30) % face_total[:, None, None, None]
    chosen = jnp.take_along_axis(face_of, picks.reshape(DEVICES, -1), 1).reshape(DEVICES, 3, ORDERS, FCAP)
    sending = jnp.where(jnp.arange(FCAP, dtype=jnp.int32)[None, None, None] < wanted[..., None], chosen, 4 * NB)
    return ((order_index + 1).reshape(ELEMS), slot_value.reshape(ELEMS), sending.reshape(DEVICES * LISTS), receive.reshape(DEVICES * 4 * NB))


def draw_orders(key, part):
    return mesh_tables(key)[0]


def draw_slots(key, part):
    return mesh_tables(key)[1]


def draw_send_faces(key, part):
    return mesh_tables(key)[2]


def draw_recv_faces(key, part):
    return mesh_tables(key)[3]


def block_levels(rng, extent, shards, least, largest):
    factor_of = 1.0
    for dim, shards_of in shards:
        draws = jax.random.uniform(jax.random.fold_in(jax.random.fold_in(rng, 6), dim), (shards_of,), jnp.float32, least / len(shards), largest / len(shards))
        factor_of = factor_of * jnp.repeat(jnp.exp(draws), extent[dim] // shards_of).reshape((-1,) + (1,) * (len(extent) - 1 - dim))
    return factor_of


def bell_draw(rng, shape, deviation, bound, cuts=(), kind=jnp.bfloat16):
    level = block_levels(rng, shape, cuts, -0.22, 0.18) if cuts else 1.0
    values = jax.random.normal(rng, shape, jnp.float32) * deviation * level
    return jnp.minimum(jnp.maximum(values, -bound), bound).astype(kind)


def setup_inputs(seed: int = 0) -> dict:
    key_list = jax.random.split(jax.random.key(seed), 12)
    return {
        "fields": bell_draw(key_list[0], (6 * NPM, ELEMS), 1.0, 6.0, ((1, 128),), jnp.float32),
        "metric": bell_draw(key_list[1], (9, ELEMS), 1.0, 5.0, ((1, 128),), jnp.float32),
        "normals": bell_draw(key_list[2], (12, ELEMS), 0.6, 3.0, ((1, 128),), jnp.float32),
        "fscale": jnp.clip(jnp.exp(math.log(4.0) - 2.0794415 * jax.random.uniform(key_list[3], (4, ELEMS), jnp.float32) ** block_levels(key_list[3], (4, ELEMS), ((1, 128),), -0.2, 0.2)), 0.5, 4.0),
        "orders": draw_orders(jax.random.fold_in(key_list[11], 71), 0),
        "slots": draw_slots(jax.random.fold_in(key_list[11], 71), 0),
        "send_faces": draw_send_faces(jax.random.fold_in(key_list[11], 71), 0),
        "recv_faces": draw_recv_faces(jax.random.fold_in(key_list[11], 71), 0),
        "dmat": bell_draw(key_list[8], (ORDERS, 3 * NPM, NPM), 0.3, 4.0, ((0, 4),), jnp.float32),
        "tmat": bell_draw(key_list[9], (ORDERS, 4 * FPTS, NPM), 0.3, 4.0, ((0, 4),), jnp.float32),
        "lmat": bell_draw(key_list[10], (ORDERS, NPM, 4 * FPTS), 0.2, 3.0, ((0, 4),), jnp.float32),
    }


exact_prec = lax.Precision.HIGHEST


def order_mask(order_index):
    node_total = (order_index + 2) * (order_index + 3) * (order_index + 4) // 6
    return (jnp.arange(NPM, dtype=jnp.int32) < node_total).astype(jnp.float32)


def cross_of(first_vec, second_vec):
    return [first_vec[1] * second_vec[2] - first_vec[2] * second_vec[1],
            first_vec[2] * second_vec[0] - first_vec[0] * second_vec[2],
            first_vec[0] * second_vec[1] - first_vec[1] * second_vec[0]]


def volume_terms(coefficients, metric_cols, deriv_mats):
    derived = jnp.einsum('anm,qms->qans', deriv_mats, coefficients, precision=exact_prec)

    def partial_of(component, direction):
        return (metric_cols[0, direction][None] * derived[component, 0]
                + metric_cols[1, direction][None] * derived[component, 1]
                + metric_cols[2, direction][None] * derived[component, 2])

    curl_h = [partial_of(5, 1) - partial_of(4, 2), partial_of(3, 2) - partial_of(5, 0), partial_of(4, 0) - partial_of(3, 1)]
    curl_e = [partial_of(2, 1) - partial_of(1, 2), partial_of(0, 2) - partial_of(2, 0), partial_of(1, 0) - partial_of(0, 1)]
    return jnp.stack(curl_h + [-value for value in curl_e], 0)


def face_flux(own_traces, neighbour, normal_cols, scale_cols):
    own_split = own_traces.reshape(6, FPTS, -1)
    far_split = neighbour.reshape(6, FPTS, -1)
    jump_e = [far_split[c] - own_split[c] for c in range(3)]
    jump_h = [far_split[c + 3] - own_split[c + 3] for c in range(3)]
    normal = [normal_cols[c] for c in range(3)]
    normal_e = normal[0] * jump_e[0] + normal[1] * jump_e[1] + normal[2] * jump_e[2]
    normal_h = normal[0] * jump_h[0] + normal[1] * jump_h[1] + normal[2] * jump_h[2]
    turn_h = cross_of(normal, jump_h)
    turn_e = cross_of(normal, jump_e)
    flux_e = [0.5 * scale_cols * (turn_h[c] + jump_e[c] - normal[c] * normal_e) for c in range(3)]
    flux_h = [0.5 * scale_cols * (-turn_e[c] + jump_h[c] - normal[c] * normal_h) for c in range(3)]
    return jnp.stack(flux_e + flux_h, 0)


def block_rhs(bucket, own_traces, neighbour, deriv_mats, lift_mat):
    slot_count = bucket.shape[1]
    coefficients = bucket[:6 * NPM].reshape(6, NPM, slot_count)
    metric_cols = bucket[6 * NPM:6 * NPM + 9].reshape(3, 3, slot_count)
    normal_cols = bucket[6 * NPM + 9:6 * NPM + 21].reshape(3, 1, 4 * slot_count)
    scale_cols = bucket[6 * NPM + 21:6 * NPM + 25].reshape(1, 4 * slot_count)
    volume = volume_terms(coefficients, metric_cols, deriv_mats)
    flux = face_flux(own_traces, neighbour, normal_cols, scale_cols).reshape(6, FPTS * 4, slot_count)
    lifted = jnp.einsum('mp,qps->qms', lift_mat, flux, precision=exact_prec)
    return (volume + lifted).reshape(6 * NPM, slot_count)


def reference(fields, metric, normals, fscale, orders, slots, send_faces, recv_faces, dmat, tmat, lmat):
    element_total = fields.shape[1]
    positions = jnp.arange(element_total, dtype=jnp.int32)
    owner = positions // E_DEV
    column = ((orders - 1) * DOMS + owner % DOMS) * NB + (owner // DOMS) * CAP + slots
    inverse = jnp.full((SLOTS,), element_total, jnp.int32).at[column].set(positions)
    payload = jnp.concatenate([fields, metric, normals, fscale], 0)
    padded = jnp.concatenate([payload, jnp.zeros((payload.shape[0], 1), jnp.float32)], 1)

    def gather_block(block_id):
        picked = lax.dynamic_slice_in_dim(inverse, block_id * NB, NB)
        return jnp.take(padded, picked, axis=1)

    def matrices(block_id):
        order_index = block_id // DOMS
        node_mask = order_mask(order_index)
        deriv_mats = dmat[order_index].reshape(3, NPM, NPM) * node_mask[None, :, None] * node_mask[None, None, :]
        trace_mat = tmat[order_index] * node_mask[None, :]
        lift_mat = lmat[order_index] * node_mask[:, None]
        return deriv_mats, trace_mat, lift_mat

    def traces_of(block_id):
        bucket = gather_block(block_id)
        trace_mat = matrices(block_id)[1]
        coefficients = bucket[:6 * NPM].reshape(6, NPM, NB)
        traced = jnp.einsum('pm,qms->qps', trace_mat, coefficients, precision=exact_prec)
        return traced.reshape(6 * FPTS, 4 * NB)

    traces = lax.map(traces_of, jnp.arange(DEVICES, dtype=jnp.int32))
    entries = jnp.arange(LISTS, dtype=jnp.int32)
    direction = entries // (ORDERS * FCAP)
    peer_group = (entries // FCAP) % ORDERS
    places = entries % FCAP
    receiver = jnp.arange(DEVICES, dtype=jnp.int32)[:, None]
    sender = peer_group[None] * DOMS + (receiver % DOMS - direction[None] + 1) % DOMS
    position = (direction[None] * ORDERS + receiver // DOMS) * FCAP + places[None]
    send_table = send_faces.reshape(DEVICES, LISTS)
    sent_face = send_table[sender, position]
    missing = DEVICES * 4 * NB
    flat_id = jnp.where(sent_face < 4 * NB, sender * (4 * NB) + sent_face, missing)
    recv_table = recv_faces.reshape(DEVICES, 4 * NB)

    def rhs_of(block_id):
        bucket = gather_block(block_id)
        deriv_mats, trace_mat, lift_mat = matrices(block_id)
        entry_ids = recv_table[block_id]
        global_ids = flat_id[block_id][jnp.minimum(entry_ids, LISTS - 1)]
        global_ids = jnp.where(entry_ids < LISTS, global_ids, missing)
        valid = (global_ids < missing).astype(jnp.float32)
        src_block = jnp.minimum(global_ids // (4 * NB), DEVICES - 1)
        face_ids = global_ids % (4 * NB)
        neighbour = traces[src_block, :, face_ids].T * valid[None]
        return block_rhs(bucket, traces[block_id], neighbour, deriv_mats, lift_mat)

    blocks = lax.map(rhs_of, jnp.arange(DEVICES, dtype=jnp.int32))
    return jnp.transpose(blocks, (1, 0, 2)).reshape(6 * NPM, SLOTS)
```

```python
import functools

import jax
import jax.numpy as jnp
from jax import lax
from jax.experimental import pallas as pl
from jax.experimental.pallas import tpu as pltpu
from jax.sharding import PartitionSpec as P

NPM = 35
FPTS = 15
ROWS = 240
COEF = 6 * NPM
LANES = 128
ITEM = 96
NODE = 40

f32 = jnp.float32
bf16 = jnp.bfloat16
VMEM = pltpu.VMEM
SMEM = pltpu.SMEM


def halves(x):
    high = x.astype(bf16)
    return high, (x - high.astype(f32)).astype(bf16)


def dot(a, b, dims):
    return lax.dot_general(a, b, (dims, ((), ())), preferred_element_type=f32)


def dot3(a, b, dims):
    return dot(a[0], b[0], dims) + (dot(a[0], b[1], dims) + dot(a[1], b[0], dims))


def exact(a, b, dims):
    return lax.dot_general(a, b, (dims, ((), ())), preferred_element_type=f32, precision=lax.Precision.HIGHEST)


def iota(shape, dim):
    return lax.broadcasted_iota(jnp.int32, shape, dim)


def ones_where(condition):
    return jnp.where(condition, 1.0, 0.0).astype(f32)


def place_kernel(capacity, fields, metric, normals, fscale, orders, slots, out, whole, payload):
    group = pl.program_id(0)

    @pl.when(group == 0)
    def _():
        whole[0:COEF] = fields[...]
        whole[COEF : COEF + 9] = metric[...]
        whole[COEF + 9 : COEF + 21] = normals[...]
        whole[COEF + 21 : COEF + 25] = fscale[...]
        whole[COEF + 25 : ROWS] = jnp.zeros((ROWS - COEF - 25, whole.shape[1]), f32)
        high, low = halves(whole[...])
        payload[0:ROWS] = high
        payload[ROWS : 2 * ROWS] = low

    column = (orders[...] - 1 - group) * capacity + slots[...]
    column = jnp.where(orders[...] - 1 == group, column, -1)
    chosen = ones_where(iota((capacity, column.shape[1]), 0) == column).astype(bf16)
    placed = dot(payload[...], chosen, ((1,), (1,)))
    out[0] = placed[0:ROWS] + placed[ROWS : 2 * ROWS]


def place(fields, metric, normals, fscale, orders, slots, groups):
    elements = fields.shape[1]
    capacity = elements // 2
    whole = lambda rows: pl.BlockSpec((rows, elements), lambda g: (0, 0))
    return pl.pallas_call(
        functools.partial(place_kernel, capacity),
        grid=(groups,),
        in_specs=[whole(COEF), whole(9), whole(12), whole(4), whole(1), whole(1)],
        out_specs=pl.BlockSpec((1, ROWS, capacity), lambda g: (g, 0, 0)),
        out_shape=jax.ShapeDtypeStruct((groups, ROWS, capacity), f32),
        scratch_shapes=[VMEM((ROWS, elements), f32), VMEM((2 * ROWS, elements), bf16)],
        name="place",
    )(fields, metric, normals, fscale, orders.reshape(1, elements), slots.reshape(1, elements))


def prepare_kernel(group, dmat, tmat, lmat, trace_rows, trace_cols, deriv, lift):
    order = group[0]
    total = (order + 2) * (order + 3) * (order + 4) // 6
    d, t, l = dmat[0], tmat[0], lmat[0]
    t = jnp.where(iota(t.shape, 1) < total, t, 0.0)
    l = jnp.where(iota(l.shape, 0) < total, l, 0.0)
    node = iota(d.shape, 0)
    node = node - NPM * (node // NPM)
    d = jnp.where((node < total) & (iota(d.shape, 1) < total), d, 0.0)

    row, col = iota((NPM, ROWS), 0), iota((NPM, ROWS), 1)
    tile = ones_where((col - NPM * (col // NPM) == row) & (col < COEF))

    shape = (4 * ITEM, 4 * FPTS)
    row, col = iota(shape, 0), iota(shape, 1)
    face, inner = row // ITEM, row % ITEM
    pick = ones_where((inner % 16 < FPTS) & (col == (inner % 16) * 4 + face))
    spread = exact(exact(pick, t, ((1,), (0,))), tile, ((1,), (0,)))
    row, col = iota(spread.shape, 0), iota(spread.shape, 1)
    spread = jnp.where((row % ITEM) // 16 == col // NPM, spread, 0.0)
    trace_rows[0], trace_rows[1] = halves(spread)

    shape = (4 * LANES, 4 * FPTS)
    row, col = iota(shape, 0), iota(shape, 1)
    face, inner = row // LANES, row % LANES
    pick = ones_where((inner < ITEM) & (inner % 16 < FPTS) & (col == (inner % 16) * 4 + face))
    spread = exact(tile, exact(pick, t, ((1,), (0,))), ((0,), (1,)))
    row, col = iota(spread.shape, 0), iota(spread.shape, 1)
    spread = jnp.where((col % LANES) // 16 == row // NPM, spread, 0.0)
    trace_cols[0], trace_cols[1] = halves(spread)

    shape = (18 * NODE, 3 * NPM)
    row, col = iota(shape, 0), iota(shape, 1)
    inner = row % NODE
    pick = ones_where((inner < NPM) & (col == (row // (6 * NODE)) * NPM + inner))
    spread = exact(exact(pick, d, ((1,), (0,))), tile, ((1,), (0,)))
    row, col = iota(spread.shape, 0), iota(spread.shape, 1)
    spread = jnp.where((row // NODE) % 6 == col // NPM, spread, 0.0)
    deriv[0], deriv[1] = halves(spread)

    shape = (NODE, NPM)
    grow = ones_where(iota(shape, 0) == iota(shape, 1))
    shape = (4 * FPTS, 64)
    row, col = iota(shape, 0), iota(shape, 1)
    pick = ones_where((col % 16 < FPTS) & (row == (col % 16) * 4 + col // 16))
    spread = exact(grow, exact(l, pick, ((1,), (0,))), ((1,), (0,)))
    lift[0], lift[1] = halves(spread)


def prepare(group, dmat, tmat, lmat):
    return pl.pallas_call(
        prepare_kernel,
        in_specs=[pl.BlockSpec(memory_space=SMEM)] + [pl.BlockSpec(memory_space=VMEM)] * 3,
        out_specs=[pl.BlockSpec(memory_space=VMEM)] * 4,
        out_shape=[
            jax.ShapeDtypeStruct((2, 4 * ITEM, ROWS), bf16),
            jax.ShapeDtypeStruct((2, ROWS, 4 * LANES), bf16),
            jax.ShapeDtypeStruct((2, 18 * NODE, ROWS), bf16),
            jax.ShapeDtypeStruct((2, NODE, 64), bf16),
        ],
        cost_estimate=pl.CostEstimate(flops=10**9, bytes_accessed=4 * 10**6, transcendentals=0),
        name="prepare",
    )(group, dmat, tmat, lmat)


def gather_rows(index, first, source, target, start, count, unroll=32):
    def body(i, carry):
        base = pl.multiple_of(i * unroll, unroll)
        for u in range(unroll):
            row = index[first + base + u]
            target[pl.ds(start + base + u, 1), :] = source[pl.ds(row, 1), :]
        return carry

    lax.fori_loop(0, count // unroll, body, 0)


def gather_lists(index, rows, items, spill):
    lists, packed = items.shape[0], items.shape[1]
    third = packed // 3
    for h in range(lists):
        gather_rows(index, h * 4 * third, rows, items.at[h], 0, packed)
        gather_rows(index, h * 4 * third + packed, rows, spill, 0, third)
        extra = spill[...]
        lane = iota(extra.shape, 1)
        for t in range(3):
            here = pl.ds(t * third, third)
            moved = pltpu.roll(extra, ITEM - 32 * t, 1)
            items[h, here, :] = jnp.where(lane < ITEM, items[h, here, :], moved)


def traces_kernel(index, bucket, trace_cols, rows, items, spill):
    groups, _, capacity = bucket.shape
    faces = 4 * groups * capacity
    weights = (trace_cols[0], trace_cols[1])
    for g in range(groups):
        columns = halves(jnp.transpose(bucket[g]))
        traced = dot3(columns, weights, ((1,), (0,)))
        for f in range(4):
            rows[pl.ds((f * groups + g) * capacity, capacity), :] = traced[:, f * LANES : (f + 1) * LANES]
    rows[pl.ds(faces, 8), :] = jnp.zeros((8, LANES), f32)
    gather_lists(index, rows, items, spill)


def lists_kernel(index, rows, items, spill):
    gather_lists(index, rows, items, spill)


def first_lists(index, bucket, trace_cols, list_size):
    groups, _, capacity = bucket.shape
    faces = 4 * groups * capacity
    packed = list_size * 3 // 4
    return pl.pallas_call(
        traces_kernel,
        in_specs=[pl.BlockSpec(memory_space=SMEM)] + [pl.BlockSpec(memory_space=VMEM)] * 2,
        out_specs=[pl.BlockSpec(memory_space=VMEM)] * 2,
        out_shape=[
            jax.ShapeDtypeStruct((faces + 8, LANES), f32),
            jax.ShapeDtypeStruct((groups, packed, LANES), f32),
        ],
        scratch_shapes=[VMEM((packed // 3, LANES), f32)],
        name="traces",
    )(index, bucket, trace_cols)


def next_lists(index, rows, groups, list_size):
    packed = list_size * 3 // 4
    return pl.pallas_call(
        lists_kernel,
        in_specs=[pl.BlockSpec(memory_space=SMEM), pl.BlockSpec(memory_space=VMEM)],
        out_specs=pl.BlockSpec(memory_space=VMEM),
        out_shape=jax.ShapeDtypeStruct((groups, packed, LANES), f32),
        scratch_shapes=[VMEM((packed // 3, LANES), f32)],
        cost_estimate=pl.CostEstimate(flops=10**7, bytes_accessed=12 * 10**6, transcendentals=0),
        name="lists",
    )(index, rows)


def face_flux(value, normal, scale):
    e, h = value[:3], value[3:]
    half = 0.5 * scale
    normal_e = normal[0] * e[0] + normal[1] * e[1] + normal[2] * e[2]
    normal_h = normal[0] * h[0] + normal[1] * h[1] + normal[2] * h[2]

    def cross(v, c):
        return normal[(c + 1) % 3] * v[(c + 2) % 3] - normal[(c + 2) % 3] * v[(c + 1) % 3]

    flux_e = [half * (cross(h, c) + e[c] - normal[c] * normal_e) for c in range(3)]
    flux_h = [half * (h[c] - cross(e, c) - normal[c] * normal_h) for c in range(3)]
    return flux_e + flux_h


def own_kernel(bucket, deriv, trace_rows, lift, part, geometry, flux):
    cols = halves(bucket[0])
    derived = dot3((deriv[0], deriv[1]), cols, ((1,), (0,)))
    row = lambda r: bucket[0, r : r + 1, :]
    metric = [[row(COEF + 3 * a + x) for x in range(3)] for a in range(3)]

    def along(component, x):
        take = lambda a: derived[(a * 6 + component) * NODE : (a * 6 + component + 1) * NODE]
        return metric[0][x] * take(0) + metric[1][x] * take(1) + metric[2][x] * take(2)

    volume = []
    for sign, first in ((1, 3), (-1, 0)):
        for c in range(3):
            y, z = (c + 1) % 3, (c + 2) % 3
            curl = along(first + z, y) - along(first + y, z)
            volume.append(curl if sign > 0 else -curl)
    geometry[...] = bucket[0, COEF + 9 : COEF + 25, :]
    own = dot3((trace_rows[0], trace_rows[1]), cols, ((1,), (0,)))
    for f in range(4):
        value = [own[f * ITEM + 16 * c : f * ITEM + 16 * (c + 1)] for c in range(6)]
        normal = [geometry[4 * c + f : 4 * c + f + 1, :] for c in range(3)]
        for c, part_of in enumerate(face_flux(value, normal, geometry[12 + f : 13 + f, :])):
            flux[c, 16 * f : 16 * (f + 1)] = part_of
    lifts = (lift[0], lift[1])
    for c in range(6):
        part[c * NODE : (c + 1) * NODE] = volume[c] - dot3(lifts, halves(flux[c]), ((1,), (0,)))


def own_part(bucket, deriv, trace_rows, lift):
    groups, _, capacity = bucket.shape
    fixed = lambda x: pl.BlockSpec(x.shape, lambda g: (0,) * x.ndim)
    return pl.pallas_call(
        own_kernel,
        grid=(groups,),
        in_specs=[pl.BlockSpec((1, ROWS, capacity), lambda g: (g, 0, 0)), fixed(deriv), fixed(trace_rows), fixed(lift)],
        out_specs=[pl.BlockSpec((6 * NODE, capacity), lambda g: (0, g)), pl.BlockSpec((16, capacity), lambda g: (0, g))],
        out_shape=[
            jax.ShapeDtypeStruct((6 * NODE, groups * capacity), f32),
            jax.ShapeDtypeStruct((16, groups * capacity), f32),
        ],
        scratch_shapes=[VMEM((6, 64, capacity), f32)],
        cost_estimate=pl.CostEstimate(flops=5 * 10**9, bytes_accessed=8 * 10**6, transcendentals=0),
        name="own_part",
    )(bucket, deriv, trace_rows, lift)


def finish_kernel(width, index, low, mid, high, part, geometry, lift, out, rows, near, flux, sems):
    step = pl.program_id(0)
    groups, packed, _ = low.shape
    third = packed // 3
    lists = 3 * groups
    slots = pl.num_programs(0) * width

    @pl.when(step == 0)
    def _():
        copies = []
        for j, source in enumerate((low, mid, high)):
            for g in range(groups):
                target = rows.at[pl.ds((j * groups + g) * packed, packed), :]
                copies.append(pltpu.make_async_copy(source.at[g], target, sems.at[j, g]))
        for copy in copies:
            copy.start()
        rows[pl.ds(lists * (packed + third), 8), :] = jnp.zeros((8, LANES), f32)
        lane = iota((third, LANES), 1)
        for n, copy in enumerate(copies):
            copy.wait()
            piece = [
                pltpu.roll(rows[pl.ds(n * packed + t * third, third), :], 32 * (t + 1), 1) for t in range(3)
            ]
            rows[pl.ds(lists * packed + n * third, third), :] = jnp.where(
                lane < 32, piece[0], jnp.where(lane < 64, piece[1], piece[2])
            )

    for f in range(4):
        gather_rows(index, f * slots + step * width, rows, near.at[f], 0, width)
    for f in range(4):
        turned = jnp.transpose(near[f])
        value = [turned[16 * c : 16 * (c + 1)] for c in range(6)]
        normal = [geometry[4 * c + f : 4 * c + f + 1, :] for c in range(3)]
        for c, part_of in enumerate(face_flux(value, normal, geometry[12 + f : 13 + f, :])):
            flux[c, 16 * f : 16 * (f + 1)] = part_of
    lifts = (lift[0], lift[1])
    for c in range(6):
        total = part[c * NODE : (c + 1) * NODE] + dot3(lifts, halves(flux[c]), ((1,), (0,)))
        out[c * NPM : (c + 1) * NPM] = total[:NPM]


def finish(index, low, mid, high, part, geometry, lift, width=256):
    groups, packed, _ = low.shape
    slots = part.shape[1]
    third = packed // 3
    block = lambda rows: pl.BlockSpec((rows, width), lambda s: (0, s))
    return pl.pallas_call(
        functools.partial(finish_kernel, width),
        grid=(slots // width,),
        in_specs=[pl.BlockSpec(memory_space=SMEM)]
        + [pl.BlockSpec(memory_space=pl.ANY)] * 3
        + [block(6 * NODE), block(16), pl.BlockSpec(lift.shape, lambda s: (0, 0, 0))],
        out_specs=block(COEF),
        out_shape=jax.ShapeDtypeStruct((COEF, slots), f32),
        scratch_shapes=[
            VMEM((3 * groups * (packed + third) + 8, LANES), f32),
            VMEM((4, width, LANES), f32),
            VMEM((6, 64, width), f32),
            pltpu.SemaphoreType.DMA((3, groups)),
        ],
        name="finish",
    )(index, low, mid, high, part, geometry, lift)


def exchange(x):
    return lax.all_to_all(x, "grp", split_axis=0, concat_axis=0, tiled=True)


def shifted(x, by):
    size = lax.axis_size("dom")
    return lax.ppermute(x, "dom", [(i, (i + by) % size) for i in range(size)])


def local(fields, metric, normals, fscale, orders, slots, send_faces, recv_faces, dmat, tmat, lmat):
    groups = lax.axis_size("grp")
    list_total = send_faces.shape[0]
    list_size = list_total // (3 * groups)
    packed = list_size * 3 // 4
    third = packed // 3
    sends = send_faces.reshape(3, groups * list_size)
    entry, place_in = recv_faces // list_size, recv_faces % list_size
    where = jnp.where(
        place_in < packed, entry * packed + place_in, 3 * groups * packed + entry * third + place_in - packed
    )
    where = jnp.where(recv_faces < list_total, where, list_total)

    bucket = exchange(place(fields, metric, normals, fscale, orders, slots, groups))
    group = lax.axis_index("grp").astype(jnp.int32).reshape(1)
    trace_rows, trace_cols, deriv, lift = prepare(group, dmat, tmat, lmat)
    rows, low = first_lists(sends[0], bucket, trace_cols, list_size)
    low = shifted(exchange(low), -1)
    high = shifted(exchange(next_lists(sends[2], rows, groups, list_size)), 1)
    mid = exchange(next_lists(sends[1], rows, groups, list_size))
    part, geometry = own_part(bucket, deriv, trace_rows, lift)
    return finish(where, low, mid, high, part, geometry, lift)


def solution(mesh):
    in_specs = (
        P(None, ("grp", "dom")),
        P(None, ("grp", "dom")),
        P(None, ("grp", "dom")),
        P(None, ("grp", "dom")),
        P(("grp", "dom")),
        P(("grp", "dom")),
        P(("grp", "dom")),
        P(("grp", "dom")),
        P("grp", None, None),
        P("grp", None, None),
        P("grp", None, None),
    )
    out_specs = P(None, ("grp", "dom"))
    return jax.shard_map(local, mesh=mesh, in_specs=in_specs, out_specs=out_specs, check_vma=False)
```
